32 devices in a mesh: seq: 4 (over z), head: 8 (over y, x, core).
Axes of the slice: x: 2, y: 2, z: 4, core: 2. Of those that a mesh axis runs over, the one named last changes fastest.
Arguments:
- queries: bfloat16 [4096, 2048], P(('seq', 'head')), may hold values from -6 to 6
- key_rows: bfloat16 [4096, 2048], P(('seq', 'head')), may hold values from -6 to 6
- value_rows: bfloat16 [4096, 2048], P(('seq', 'head')), may hold values from -6 to 6
- ridge_diag: float32 [16, 128], replicated, may hold values from 0.5 to 4
Outputs:
- mixed: bfloat16 [4096, 2048], P(('seq', 'head'))
The draws below stay inside these ranges and needn't reach their ends.
All inputs are finite; a program needn't handle non-finite values.
Results may differ from the reference program's by a relative error of at most 0.0075.
The reference program's roundings to bfloat16 on the way (of `q_unit` and `k_unit`) count: a program that leaves them out, or rounds other values in their place, can miss the bound.
Values may be sent and summed in bfloat16 or wider, within the bound.
A program may use at most 64 MiB of HBM per device.

```python
import math
import jax
import jax.numpy as jnp
from jax import lax

HEADS = 16
DK = 128
GROUP = 64
TOK_DEV = 128
TOKENS = 4096


def draw_key_rows(key, part):
    rank_count = max(DK // 8, 2)
    switch_len = 16 * GROUP
    segment_count = TOKENS // switch_len + 2
    shift_key = jax.random.fold_in(key, 11)
    basis_key = jax.random.fold_in(key, 12)
    coeff_key = jax.random.fold_in(key, 13)
    noise_key = jax.random.fold_in(key, 14)
    shift_by = jax.random.randint(shift_key, (HEADS,), 0, switch_len, dtype=jnp.int32)
    positions = jnp.arange(TOKENS, dtype=jnp.int32)
    segment = (positions[:, None] + shift_by[None, :]) // switch_len
    basis = jax.random.normal(basis_key, (rank_count, HEADS, segment_count, DK), jnp.float32)
    coeffs = jax.random.normal(coeff_key, (TOKENS, HEADS, rank_count), jnp.float32)
    noise = 0.05 * jax.random.normal(noise_key, (TOKENS, HEADS, DK), jnp.float32)
    grade = jnp.exp(-jnp.log(10.0) * jnp.arange(rank_count, dtype=jnp.float32) / (rank_count - 1))
    head_index = jnp.arange(HEADS, dtype=jnp.int32)[None, :]
    total = noise
    for which in range(rank_count):
        picked = basis[which][head_index, segment]
        total = total + (coeffs[:, :, which] * grade[which])[:, :, None] * picked
    return jnp.clip(total, -6.0, 6.0).reshape(TOKENS, HEADS * DK).astype(jnp.bfloat16)


def shard_levels(own_key, extent, pieces, low, largest):
    factor_of, own = 1.0, jax.random.fold_in(own_key, 6)
    for dim, parts in pieces:
        steps = jnp.exp(jax.random.uniform(jax.random.fold_in(own, dim), (parts,), jnp.float32, low / len(pieces), largest / len(pieces)))
        factor_of = factor_of * jnp.repeat(steps, extent[dim] // parts).reshape([-1 if axis == dim else 1 for axis in range(len(extent))])
    return factor_of


def gaussian(key, shape, deviation, most, cuts=(), kind=jnp.bfloat16):
    entries = deviation * jax.random.normal(key, shape, jnp.float32)
    if cuts:
        entries = entries * shard_levels(key, shape, cuts, -0.22, 0.18)
    return jnp.clip(entries, -most, most).astype(kind)


def setup_inputs(seed: int = 0) -> dict:
    seeds = jax.random.split(jax.random.key(seed), 5)
    queries = gaussian(seeds[0], (TOKENS, HEADS * DK), 1.0, 6.0, ((0, 32),))
    key_rows = draw_key_rows(jax.random.fold_in(seeds[4], 71), 0)
    value_rows = gaussian(seeds[2], (TOKENS, HEADS * DK), 1.0, 6.0, ((0, 32),))
    ridge_diag = jnp.clip(jnp.exp(jax.random.uniform(seeds[3], (HEADS, DK), jnp.float32, math.log(0.5), math.log(4.0))), 0.5, 4.0)
    return dict(queries=queries, key_rows=key_rows, value_rows=value_rows, ridge_diag=ridge_diag)


epsilon = 1e-06
highest = lax.Precision.HIGHEST

def unit_rows(matrix):
    values_f = matrix.astype(jnp.float32)
    scale_back = lax.rsqrt(lax.optimization_barrier(jnp.sum(values_f * values_f, axis=-1, keepdims=True)) + epsilon)
    return (values_f * scale_back).astype(jnp.bfloat16)

def reference(queries, key_rows, value_rows, ridge_diag):
    per_block = TOK_DEV // GROUP
    block_count = TOKENS // TOK_DEV

    def head_out(head_index):
        offset = head_index * DK
        q_head = lax.dynamic_slice_in_dim(queries, offset, DK, 1)
        k_head = lax.dynamic_slice_in_dim(key_rows, offset, DK, 1)
        v_head = lax.dynamic_slice_in_dim(value_rows, offset, DK, 1)
        ridge_here = lax.dynamic_slice_in_dim(ridge_diag, head_index, 1, 0)[0]
        q_unit = unit_rows(q_head).reshape(block_count, per_block, GROUP, DK)
        k_unit = unit_rows(k_head).reshape(block_count, per_block, GROUP, DK)
        v_block = v_head.reshape(block_count, per_block, GROUP, DK)

        def advance(running, inputs_now):
            gram_run, vk_run = running
            q_now, k_now, v_now = inputs_now
            k_f = k_now.astype(jnp.float32)
            v_f = v_now.astype(jnp.float32)
            group_gram = jnp.einsum('cti,ctj->cij', k_f, k_f, precision=highest)
            group_vk = jnp.einsum('ctv,ctk->cvk', v_f, k_f, precision=highest)
            gram_inc = jnp.cumsum(group_gram, axis=0)
            vk_inc = jnp.cumsum(group_vk, axis=0)
            gram_start = gram_run + gram_inc - group_gram
            vk_start = vk_run + vk_inc - group_vk
            system = gram_start + jnp.diag(ridge_here)
            factor = jnp.linalg.cholesky(system)
            targets = jnp.swapaxes(q_now.astype(jnp.float32), -1, -2)
            half_solved = jax.scipy.linalg.solve_triangular(factor, targets, lower=True)
            solved = jax.scipy.linalg.solve_triangular(factor, half_solved, lower=True, trans=1)
            carried = jnp.einsum('cvk,ckt->ctv', vk_start, solved, precision=highest)
            scores = jnp.einsum('csk,ckt->cts', k_f, solved, precision=highest)
            causal = jnp.arange(GROUP)[None, :] <= jnp.arange(GROUP)[:, None]
            within = jnp.einsum('cts,csv->ctv', jnp.where(causal[None], scores, 0.0), v_f, precision=highest)
            result = (carried + within).astype(jnp.bfloat16)
            return ((gram_run + gram_inc[-1], vk_run + vk_inc[-1]), result)
        zero_state = jnp.zeros((DK, DK), jnp.float32)
        _, outputs = lax.scan(advance, (zero_state, zero_state), (q_unit, k_unit, v_block))
        return outputs.reshape(TOKENS, DK)
    stacked = lax.map(head_out, jnp.arange(HEADS, dtype=jnp.int32))
    return jnp.transpose(stacked, (1, 0, 2)).reshape(TOKENS, HEADS * DK)
```

```python
import functools

import jax
import jax.numpy as jnp
from jax import lax
from jax.experimental import pallas as pl
from jax.experimental.pallas import tpu as pltpu
from jax.sharding import PartitionSpec as P

DK = 128
GROUP = 64
EDGE = 32
PACK = DK // EDGE
EPS = 1e-06
F32 = jnp.float32
BF16 = jnp.bfloat16


def unit(rows):
    wide = rows.astype(F32)
    back = lax.rsqrt(jnp.sum(wide * wide, axis=-1, keepdims=True) + EPS)
    return (wide * back).astype(BF16)


def split3(value):
    high = value.astype(BF16)
    rest = value - high.astype(F32)
    mid = rest.astype(BF16)
    low = (rest - mid.astype(F32)).astype(BF16)
    return high, mid, low


def dot(left, right, contract):
    return lax.dot_general(left, right, ((contract[:1], contract[1:]), ((), ())), preferred_element_type=F32)


def left_stack(parts):
    high, mid, low = parts
    return jnp.concatenate([high, high, mid, high, low, mid], axis=0)


def right_stack(parts):
    high, mid, low = parts
    return jnp.concatenate([high, mid, high, low, high, mid], axis=0)


def sweep_pack(rows, lane, sub):
    base = (lane // EDGE) * EDGE
    within = lane - base
    for j in range(EDGE):
        at, inner = j // 8, j % 8
        column = within == j
        pick = base + j
        pivot_row = jnp.broadcast_to(rows[at][inner : inner + 1, :], rows[at].shape)
        pivot = jnp.take_along_axis(pivot_row, pick, axis=1, mode="promise_in_bounds")
        scaled = jnp.where(column, -1.0, pivot_row) * (1.0 / pivot)
        fresh = []
        for v, block in enumerate(rows):
            col = jnp.take_along_axis(block, pick, axis=1, mode="promise_in_bounds")
            gone = column
            if v == at:
                here = sub == inner
                col = jnp.where(here, -1.0, col)
                gone = jnp.logical_or(column, here)
            fresh.append(jnp.where(gone, 0.0, block) - col * scaled)
        rows = fresh
    return rows


def totals_kernel(k_ref, v_ref, ku_ref, tot_ref):
    heads = k_ref.shape[1] // DK
    for h in range(heads):
        cols = slice(h * DK, (h + 1) * DK)
        ku = unit(k_ref[:, cols])
        ku_ref[:, cols] = ku
        both = jnp.concatenate([ku, v_ref[:, cols]], axis=1)
        tot_ref[h] = dot(ku, both, (0, 0))


def invert_all(sys_ref, pinv_ref):
    count = sys_ref.shape[0]
    packs = count // PACK
    lane = lax.broadcasted_iota(jnp.int32, (8, DK), 1)
    sub = lax.broadcasted_iota(jnp.int32, (8, DK), 0)
    lane32 = lax.broadcasted_iota(jnp.int32, (EDGE, DK), 1)
    sub32 = lax.broadcasted_iota(jnp.int32, (EDGE, DK), 0)
    row128 = lax.broadcasted_iota(jnp.int32, (DK, DK), 0) // EDGE
    lane128 = lax.broadcasted_iota(jnp.int32, (DK, DK), 1) // EDGE

    def panel(p, carry):
        start = pl.multiple_of(p * EDGE, EDGE)
        all_rows = []
        for g in range(packs):
            packed = None
            for k in range(PACK):
                piece = sys_ref[g * PACK + k, pl.ds(start, EDGE), :]
                piece = pltpu.roll(piece, lax.rem((k - p) * EDGE + DK, DK), 1)
                packed = piece if packed is None else jnp.where(lane32 // EDGE == k, piece, packed)
            all_rows.append([packed[8 * v : 8 * v + 8, :] for v in range(EDGE // 8)])
        for g in range(packs):
            done = sweep_pack(all_rows[g], lane, sub)
            pinv_ref[g] = jnp.concatenate(done, axis=0)

        mine = lane32 // EDGE == p
        diag = lane32 - p * EDGE == sub32
        cleared = jnp.logical_or(row128 == p, lane128 == p)

        def update(g, carry):
            inverse = left_stack(split3(pinv_ref[g]))
            for k in range(PACK):
                s = g * PACK + k
                rows = sys_ref[s, pl.ds(start, EDGE), :]
                rows = jnp.where(mine, jnp.where(diag, -1.0, 0.0), rows)
                parts = split3(rows)
                full = dot(inverse, right_stack(parts), (0, 0))
                scaled = full[k * EDGE : (k + 1) * EDGE, :]
                change = dot(left_stack(parts), right_stack(split3(scaled)), (0, 0))
                sys_ref[s] = jnp.where(cleared, 0.0, sys_ref[s]) + change
            return carry

        return lax.fori_loop(0, packs, update, carry)

    lax.fori_loop(0, PACK, panel, 0)


def build_systems(ku_ref, v_ref, pre_ref, ridge_ref, sys_ref, vk_ref):
    groups = ku_ref.shape[0] // GROUP
    heads = ku_ref.shape[1] // DK
    eye = lax.broadcasted_iota(jnp.int32, (DK, DK), 0) == lax.broadcasted_iota(jnp.int32, (DK, DK), 1)
    for h in range(heads):
        cols = slice(h * DK, (h + 1) * DK)
        ridge = jnp.where(eye, ridge_ref[h : h + 1, :], 0.0)

        def step(c, run):
            rows = pl.ds(pl.multiple_of(c * GROUP, GROUP), GROUP)
            sys_ref[h * groups + c] = run[:, :DK] + ridge
            vk_ref[h * groups + c] = run[:, DK:]
            ku = ku_ref[rows, cols]
            return run + dot(ku, jnp.concatenate([ku, v_ref[rows, cols]], axis=1), (0, 0))

        lax.fori_loop(0, groups, step, pre_ref[h])


def finish(q_ref, ku_ref, v_ref, sys_ref, vk_ref, out_ref):
    groups = ku_ref.shape[0] // GROUP
    heads = ku_ref.shape[1] // DK
    causal = lax.broadcasted_iota(jnp.int32, (GROUP, GROUP), 1) <= lax.broadcasted_iota(jnp.int32, (GROUP, GROUP), 0)
    for h in range(heads):
        cols = slice(h * DK, (h + 1) * DK)

        def step(c, carry):
            rows = pl.ds(pl.multiple_of(c * GROUP, GROUP), GROUP)
            qu = unit(q_ref[rows, cols])
            high, mid, low = split3(sys_ref[h * groups + c])
            solved = -(dot(qu, high, (1, 0)) + (dot(qu, mid, (1, 0)) + dot(qu, low, (1, 0))))
            shigh, smid, slow = split3(solved)
            vhigh, vmid, vlow = split3(vk_ref[h * groups + c])
            carried = dot(shigh, vhigh, (1, 0)) + (
                dot(shigh, vmid, (1, 0)) + dot(smid, vhigh, (1, 0)) + (
                    dot(smid, vmid, (1, 0)) + dot(shigh, vlow, (1, 0)) + dot(slow, vhigh, (1, 0))))
            ku = ku_ref[rows, cols]
            scores = dot(shigh, ku, (1, 1)) + (dot(smid, ku, (1, 1)) + dot(slow, ku, (1, 1)))
            chigh, cmid, clow = split3(jnp.where(causal, scores, 0.0))
            vb = v_ref[rows, cols]
            inner = dot(chigh, vb, (1, 0)) + (dot(cmid, vb, (1, 0)) + dot(clow, vb, (1, 0)))
            out_ref[rows, cols] = (carried + inner).astype(BF16)
            return carry

        lax.fori_loop(0, groups, step, 0)


def solve_kernel(q_ref, ku_ref, v_ref, pre_ref, ridge_ref, out_ref, sys_ref, vk_ref, pinv_ref):
    build_systems(ku_ref, v_ref, pre_ref, ridge_ref, sys_ref, vk_ref)
    invert_all(sys_ref, pinv_ref)
    finish(q_ref, ku_ref, v_ref, sys_ref, vk_ref, out_ref)


def body(queries, key_rows, value_rows, ridge_diag):
    owners = lax.axis_size("head")
    heads = queries.shape[1] // DK // owners
    width = heads * DK

    def spread(rows):
        return lax.all_to_all(rows, "head", split_axis=1, concat_axis=0, tiled=True)

    k_all, v_all, q_all = spread(key_rows), spread(value_rows), spread(queries)
    tokens = k_all.shape[0]
    systems = heads * (tokens // GROUP)
    vmem = pl.BlockSpec(memory_space=pltpu.VMEM)
    ku, total = pl.pallas_call(
        totals_kernel,
        out_shape=(
            jax.ShapeDtypeStruct((tokens, width), BF16),
            jax.ShapeDtypeStruct((heads, DK, 2 * DK), F32),
        ),
        in_specs=[vmem] * 2,
        out_specs=(vmem, vmem),
    )(k_all, v_all)
    gathered = lax.all_gather(total, "seq")
    mine = lax.axis_index("seq")
    before = jnp.arange(lax.axis_size("seq")) < mine
    pre = jnp.sum(jnp.where(before[:, None, None, None], gathered, 0.0), axis=0)
    ridge = lax.dynamic_slice_in_dim(ridge_diag, lax.axis_index("head") * heads, heads, 0)
    out = pl.pallas_call(
        solve_kernel,
        out_shape=jax.ShapeDtypeStruct((tokens, width), BF16),
        in_specs=[vmem] * 5,
        out_specs=vmem,
        scratch_shapes=[
            pltpu.VMEM((systems, DK, DK), F32),
            pltpu.VMEM((systems, DK, DK), F32),
            pltpu.VMEM((systems // PACK, EDGE, DK), F32),
        ],
        compiler_params=pltpu.CompilerParams(vmem_limit_bytes=48 * 1024 * 1024),
    )(q_all, ku, v_all, pre, ridge)
    return lax.all_to_all(out, "head", split_axis=0, concat_axis=1, tiled=True)


def solution(mesh):
    in_specs = (P(("seq", "head"), None), P(("seq", "head"), None), P(("seq", "head"), None), P())
    out_specs = P(("seq", "head"), None)
    return jax.shard_map(body, mesh=mesh, in_specs=in_specs, out_specs=out_specs, check_vma=False)
```

```python
import functools

import jax
import jax.numpy as jnp
from jax import lax
from jax.experimental import pallas as pl
from jax.experimental.pallas import tpu as pltpu
from jax.sharding import PartitionSpec as P

DK = 128
GROUP = 64
EDGE = 32
PACK = DK // EDGE
STEP_PACKS = 2
STEP_GROUPS = 4
EPS = 1e-06
F32 = jnp.float32
BF16 = jnp.bfloat16


def unit(rows):
    wide = rows.astype(F32)
    back = lax.rsqrt(jnp.sum(wide * wide, axis=-1, keepdims=True) + EPS)
    return (wide * back).astype(BF16)


def split3(value):
    high = value.astype(BF16)
    rest = value - high.astype(F32)
    mid = rest.astype(BF16)
    low = (rest - mid.astype(F32)).astype(BF16)
    return high, mid, low


def dot(left, right, contract):
    return lax.dot_general(left, right, ((contract[:1], contract[1:]), ((), ())), preferred_element_type=F32)


def left_stack(parts):
    high, mid, low = parts
    return jnp.concatenate([high, high, mid, high, low, mid], axis=0)


def right_stack(parts):
    high, mid, low = parts
    return jnp.concatenate([high, mid, high, low, high, mid], axis=0)


def sweep_pack(rows, lane, sub):
    base = (lane // EDGE) * EDGE
    within = lane - base

    def take(block, pick):
        return jnp.take_along_axis(block, pick, axis=1, mode="promise_in_bounds")

    for j in range(0, EDGE, 2):
        at, inner = j // 8, j % 8
        first, second = within == j, within == j + 1
        either = jnp.logical_or(first, second)
        pick1, pick2 = base + j, base + j + 1
        row1 = jnp.broadcast_to(rows[at][inner : inner + 1, :], rows[at].shape)
        row2 = jnp.broadcast_to(rows[at][inner + 1 : inner + 2, :], rows[at].shape)
        a, b, d = take(row1, pick1), take(row1, pick2), take(row2, pick2)
        inv1 = 1.0 / a
        ratio = b * inv1
        inv2 = 1.0 / (d - b * ratio)
        scaled1 = jnp.where(first, -1.0, row1) * inv1
        scaled2 = jnp.where(second, -1.0, jnp.where(first, 0.0, row2) - b * scaled1) * inv2
        scaled1 = jnp.where(second, 0.0, scaled1)
        fresh = []
        for v, block in enumerate(rows):
            col1, col2 = take(block, pick1), take(block, pick2)
            gone = either
            if v == at:
                here1, here2 = sub == inner, sub == inner + 1
                col1 = jnp.where(here1, -1.0, col1)
                col2 = jnp.where(here2, -1.0, jnp.where(here1, 0.0, col2) - col1 * ratio)
                col1 = jnp.where(here2, 0.0, col1)
                gone = jnp.logical_or(either, jnp.logical_or(here1, here2))
            else:
                col2 = col2 - col1 * ratio
            fresh.append(jnp.where(gone, 0.0, block) - col1 * scaled1 - col2 * scaled2)
        rows = fresh
    return rows


def totals_kernel(k_ref, v_ref, ku_ref, tot_ref):
    heads = k_ref.shape[1] // DK
    for h in range(heads):
        cols = slice(h * DK, (h + 1) * DK)
        ku = unit(k_ref[:, cols])
        ku_ref[:, cols] = ku
        both = jnp.concatenate([ku, v_ref[:, cols]], axis=1)
        tot_ref[h] = dot(ku, both, (0, 0))


def invert_all(sys_ref, pinv_ref):
    count = sys_ref.shape[0]
    packs = count // PACK
    lane = lax.broadcasted_iota(jnp.int32, (8, DK), 1)
    sub = lax.broadcasted_iota(jnp.int32, (8, DK), 0)
    lane32 = lax.broadcasted_iota(jnp.int32, (EDGE, DK), 1)
    sub32 = lax.broadcasted_iota(jnp.int32, (EDGE, DK), 0)
    row128 = lax.broadcasted_iota(jnp.int32, (DK, DK), 0) // EDGE
    lane128 = lax.broadcasted_iota(jnp.int32, (DK, DK), 1) // EDGE

    def panel(p, carry):
        start = pl.multiple_of(p * EDGE, EDGE)
        all_rows = []
        for g in range(packs):
            packed = None
            for k in range(PACK):
                piece = sys_ref[g * PACK + k, pl.ds(start, EDGE), :]
                piece = pltpu.roll(piece, lax.rem((k - p) * EDGE + DK, DK), 1)
                packed = piece if packed is None else jnp.where(lane32 // EDGE == k, piece, packed)
            all_rows.append([packed[8 * v : 8 * v + 8, :] for v in range(EDGE // 8)])
        for g in range(packs):
            done = sweep_pack(all_rows[g], lane, sub)
            pinv_ref[g] = jnp.concatenate(done, axis=0)

        mine = lane32 // EDGE == p
        diag = lane32 - p * EDGE == sub32
        cleared = jnp.logical_or(row128 == p, lane128 == p)

        def update(turn, carry):
            batch = [turn * STEP_PACKS + i for i in range(STEP_PACKS)]
            rows, inverses = [], []
            for g in batch:
                inverses.append(jnp.transpose(left_stack(split3(pinv_ref[g]))))
                for k in range(PACK):
                    rows.append(sys_ref[g * PACK + k, pl.ds(start, EDGE), :])
            rows = [split3(jnp.where(mine, jnp.where(diag, -1.0, 0.0), r)) for r in rows]
            scaled = []
            for i in range(STEP_PACKS):
                for k in range(PACK):
                    left = inverses[i][k * EDGE : (k + 1) * EDGE, :]
                    scaled.append(dot(left, right_stack(rows[i * PACK + k]), (1, 0)))
            change = [dot(left_stack(r), right_stack(split3(t)), (0, 0)) for r, t in zip(rows, scaled)]
            for i, c in enumerate(change):
                s = turn * STEP_PACKS * PACK + i
                sys_ref[s] = jnp.where(cleared, 0.0, sys_ref[s]) + c
            return carry

        return lax.fori_loop(0, packs // STEP_PACKS, update, carry)

    lax.fori_loop(0, PACK, panel, 0)


def build_systems(ku_ref, v_ref, pre_ref, ridge_ref, sys_ref, vk_ref):
    groups = ku_ref.shape[0] // GROUP
    heads = ku_ref.shape[1] // DK
    eye = lax.broadcasted_iota(jnp.int32, (DK, DK), 0) == lax.broadcasted_iota(jnp.int32, (DK, DK), 1)
    for h in range(heads):
        cols = slice(h * DK, (h + 1) * DK)
        ridge = jnp.where(eye, ridge_ref[h : h + 1, :], 0.0)

        def step(turn, run):
            adds = []
            for i in range(STEP_GROUPS):
                rows = pl.ds(pl.multiple_of((turn * STEP_GROUPS + i) * GROUP, GROUP), GROUP)
                ku = ku_ref[rows, cols]
                adds.append(dot(ku, jnp.concatenate([ku, v_ref[rows, cols]], axis=1), (0, 0)))
            for i in range(STEP_GROUPS):
                c = turn * STEP_GROUPS + i
                sys_ref[h * groups + c] = run[:, :DK] + ridge
                vk_ref[h * groups + c] = run[:, DK:]
                run = run + adds[i]
            return run

        lax.fori_loop(0, groups // STEP_GROUPS, step, pre_ref[h])


def finish(q_ref, ku_ref, v_ref, sys_ref, vk_ref, out_ref):
    groups = ku_ref.shape[0] // GROUP
    heads = ku_ref.shape[1] // DK
    sub = lax.broadcasted_iota(jnp.int32, (GROUP, 2 * GROUP), 0)
    lane = lax.broadcasted_iota(jnp.int32, (GROUP, 2 * GROUP), 1)
    twice = lane >= GROUP
    causal = jnp.where(twice, lane - GROUP, lane) <= sub
    for h in range(heads):
        cols = slice(h * DK, (h + 1) * DK)

        def step(turn, carry):
            places = [turn * STEP_GROUPS + i for i in range(STEP_GROUPS)]
            rows = [pl.ds(pl.multiple_of(c * GROUP, GROUP), GROUP) for c in places]
            solved = []
            for c, r in zip(places, rows):
                qu = unit(q_ref[r, cols])
                full = jnp.concatenate(split3(sys_ref[h * groups + c]), axis=0)
                solved.append(split3(-dot(jnp.concatenate([qu, qu, qu], axis=1), full, (1, 0))))
            scores, carried = [], []
            for c, r, (high, mid, low) in zip(places, rows, solved):
                ku = ku_ref[r, cols]
                ku = jnp.concatenate([ku, ku], axis=0)
                ku = jnp.concatenate([ku, ku, ku], axis=1)
                scores.append(dot(jnp.concatenate([high, mid, low], axis=1), ku, (1, 1)))
                left = jnp.concatenate([high, high, mid, high, low, mid], axis=1)
                carried.append(dot(left, right_stack(split3(vk_ref[h * groups + c])), (1, 0)))
            results = []
            for r, score, carry_in in zip(rows, scores, carried):
                score = jnp.where(causal, score, 0.0)
                high = score.astype(BF16).astype(F32)
                both = jnp.where(twice, score - high, high).astype(BF16)
                vb = v_ref[r, cols]
                inner = dot(both, jnp.concatenate([vb, vb], axis=0), (1, 0))
                results.append((carry_in + inner).astype(BF16))
            for r, result in zip(rows, results):
                out_ref[r, cols] = result
            return carry

        lax.fori_loop(0, groups // STEP_GROUPS, step, 0)


def solve_kernel(q_ref, ku_ref, v_ref, pre_ref, ridge_ref, out_ref, sys_ref, vk_ref, pinv_ref):
    build_systems(ku_ref, v_ref, pre_ref, ridge_ref, sys_ref, vk_ref)
    invert_all(sys_ref, pinv_ref)
    finish(q_ref, ku_ref, v_ref, sys_ref, vk_ref, out_ref)


def body(queries, key_rows, value_rows, ridge_diag):
    owners = lax.axis_size("head")
    heads = queries.shape[1] // DK // owners
    width = heads * DK

    def spread(rows):
        return lax.all_to_all(rows, "head", split_axis=1, concat_axis=0, tiled=True)

    k_all, v_all, q_all = spread(key_rows), spread(value_rows), spread(queries)
    tokens = k_all.shape[0]
    systems = heads * (tokens // GROUP)
    vmem = pl.BlockSpec(memory_space=pltpu.VMEM)
    ku, total = pl.pallas_call(
        totals_kernel,
        out_shape=(
            jax.ShapeDtypeStruct((tokens, width), BF16),
            jax.ShapeDtypeStruct((heads, DK, 2 * DK), F32),
        ),
        in_specs=[vmem] * 2,
        out_specs=(vmem, vmem),
    )(k_all, v_all)
    gathered = lax.all_gather(total, "seq")
    mine = lax.axis_index("seq")
    before = jnp.arange(lax.axis_size("seq")) < mine
    pre = jnp.sum(jnp.where(before[:, None, None, None], gathered, 0.0), axis=0)
    ridge = lax.dynamic_slice_in_dim(ridge_diag, lax.axis_index("head") * heads, heads, 0)
    out = pl.pallas_call(
        solve_kernel,
        out_shape=jax.ShapeDtypeStruct((tokens, width), BF16),
        in_specs=[vmem] * 5,
        out_specs=vmem,
        scratch_shapes=[
            pltpu.VMEM((systems, DK, DK), F32),
            pltpu.VMEM((systems, DK, DK), F32),
            pltpu.VMEM((systems // PACK, EDGE, DK), F32),
        ],
        compiler_params=pltpu.CompilerParams(vmem_limit_bytes=48 * 1024 * 1024),
    )(q_all, ku, v_all, pre, ridge)
    return lax.all_to_all(out, "head", split_axis=0, concat_axis=1, tiled=True)


def solution(mesh):
    in_specs = (P(("seq", "head"), None), P(("seq", "head"), None), P(("seq", "head"), None), P())
    out_specs = P(("seq", "head"), None)
    return jax.shard_map(body, mesh=mesh, in_specs=in_specs, out_specs=out_specs, check_vma=False)
```

```python
import functools

import jax
import jax.numpy as jnp
from jax import lax
from jax.experimental import pallas as pl
from jax.experimental.pallas import tpu as pltpu
from jax.sharding import PartitionSpec as P

DK = 128
GROUP = 64
EDGE = 32
PACK = DK // EDGE
STEP_PACKS = 2
STEP_GROUPS = 4
EPS = 1e-06
F32 = jnp.float32
BF16 = jnp.bfloat16


def unit(rows):
    wide = rows.astype(F32)
    back = lax.rsqrt(jnp.sum(wide * wide, axis=-1, keepdims=True) + EPS)
    return (wide * back).astype(BF16)


def split3(value):
    high = value.astype(BF16)
    rest = value - high.astype(F32)
    mid = rest.astype(BF16)
    low = (rest - mid.astype(F32)).astype(BF16)
    return high, mid, low


def dot(left, right, contract):
    return lax.dot_general(left, right, ((contract[:1], contract[1:]), ((), ())), preferred_element_type=F32)


def left_stack(parts):
    high, mid, low = parts
    return jnp.concatenate([high, high, mid, high, low, mid], axis=0)


def right_stack(parts):
    high, mid, low = parts
    return jnp.concatenate([high, mid, high, low, high, mid], axis=0)


def sweep_pack(rows, lane, sub):
    base = (lane // EDGE) * EDGE
    within = lane - base

    def take(block, pick):
        return jnp.take_along_axis(block, pick, axis=1, mode="promise_in_bounds")

    for j in range(0, EDGE, 2):
        at, inner = j // 8, j % 8
        first, second = within == j, within == j + 1
        either = jnp.logical_or(first, second)
        pick1, pick2 = base + j, base + j + 1
        row1 = jnp.broadcast_to(rows[at][inner : inner + 1, :], rows[at].shape)
        row2 = jnp.broadcast_to(rows[at][inner + 1 : inner + 2, :], rows[at].shape)
        a, b, d = take(row1, pick1), take(row1, pick2), take(row2, pick2)
        inv1 = 1.0 / a
        ratio = b * inv1
        inv2 = 1.0 / (d - b * ratio)
        scaled1 = jnp.where(first, -1.0, row1) * inv1
        scaled2 = jnp.where(second, -1.0, jnp.where(first, 0.0, row2) - b * scaled1) * inv2
        scaled1 = jnp.where(second, 0.0, scaled1)
        fresh = []
        for v, block in enumerate(rows):
            col1, col2 = take(block, pick1), take(block, pick2)
            gone = either
            if v == at:
                here1, here2 = sub == inner, sub == inner + 1
                col1 = jnp.where(here1, -1.0, col1)
                col2 = jnp.where(here2, -1.0, jnp.where(here1, 0.0, col2) - col1 * ratio)
                col1 = jnp.where(here2, 0.0, col1)
                gone = jnp.logical_or(either, jnp.logical_or(here1, here2))
            else:
                col2 = col2 - col1 * ratio
            fresh.append(jnp.where(gone, 0.0, block) - col1 * scaled1 - col2 * scaled2)
        rows = fresh
    return rows


def invert_all(sys_ref, pinv_ref):
    count = sys_ref.shape[0]
    packs = count // PACK
    lane = lax.broadcasted_iota(jnp.int32, (8, DK), 1)
    sub = lax.broadcasted_iota(jnp.int32, (8, DK), 0)
    lane32 = lax.broadcasted_iota(jnp.int32, (EDGE, DK), 1)
    sub32 = lax.broadcasted_iota(jnp.int32, (EDGE, DK), 0)
    row128 = lax.broadcasted_iota(jnp.int32, (DK, DK), 0) // EDGE
    lane128 = lax.broadcasted_iota(jnp.int32, (DK, DK), 1) // EDGE

    def panel(p, carry):
        start = pl.multiple_of(p * EDGE, EDGE)
        all_rows = []
        for g in range(packs):
            packed = None
            for k in range(PACK):
                piece = sys_ref[g * PACK + k, pl.ds(start, EDGE), :]
                piece = pltpu.roll(piece, lax.rem((k - p) * EDGE + DK, DK), 1)
                packed = piece if packed is None else jnp.where(lane32 // EDGE == k, piece, packed)
            all_rows.append([packed[8 * v : 8 * v + 8, :] for v in range(EDGE // 8)])
        for g in range(packs):
            done = sweep_pack(all_rows[g], lane, sub)
            pinv_ref[g] = jnp.concatenate(done, axis=0)

        mine = lane32 // EDGE == p
        diag = lane32 - p * EDGE == sub32
        cleared = jnp.logical_or(row128 == p, lane128 == p)

        def update(turn, carry):
            batch = [turn * STEP_PACKS + i for i in range(STEP_PACKS)]
            rows, inverses = [], []
            for g in batch:
                inverses.append(jnp.transpose(left_stack(split3(pinv_ref[g]))))
                for k in range(PACK):
                    rows.append(sys_ref[g * PACK + k, pl.ds(start, EDGE), :])
            rows = [split3(jnp.where(mine, jnp.where(diag, -1.0, 0.0), r)) for r in rows]
            scaled = []
            for i in range(STEP_PACKS):
                for k in range(PACK):
                    left = inverses[i][k * EDGE : (k + 1) * EDGE, :]
                    scaled.append(dot(left, right_stack(rows[i * PACK + k]), (1, 0)))
            change = [dot(left_stack(r), right_stack(split3(t)), (0, 0)) for r, t in zip(rows, scaled)]
            for i, c in enumerate(change):
                s = turn * STEP_PACKS * PACK + i
                sys_ref[s] = jnp.where(cleared, 0.0, sys_ref[s]) + c
            return carry

        return lax.fori_loop(0, packs // STEP_PACKS, update, carry)

    lax.fori_loop(0, PACK, panel, 0)


def whole_kernel(
    owners, shards, q_hbm, k_hbm, v_hbm, ridge_ref, out_hbm,
    q_all, k_all, v_all, sys_ref, vk_ref, pinv_ref, stage, gram_total, vk_total, gram_slots, vk_slots,
    send_sems, recv_sems, local_sems, out_send, out_recv, out_local, gram_send, gram_recv, vk_send, vk_recv,
):
    me, shard = lax.axis_index("head"), lax.axis_index("seq")
    rows_each = q_hbm.shape[0]
    width = q_all.shape[1]
    heads = width // DK
    per_source = rows_each // GROUP
    groups = owners * per_source
    moved = ((k_hbm, k_all), (v_hbm, v_all), (q_hbm, q_all))

    def rows_of(source):
        return pl.ds(pl.multiple_of(source * rows_each, rows_each), rows_each)

    def cols_of(owner):
        return pl.ds(pl.multiple_of(owner * width, width), width)

    def incoming(kind, source):
        return pltpu.make_async_remote_copy(
            src_ref=moved[kind][0].at[:, cols_of(source)],
            dst_ref=moved[kind][1].at[rows_of(source), :],
            send_sem=send_sems.at[kind, source],
            recv_sem=recv_sems.at[kind, source],
            device_id={"head": source},
            device_id_type=pl.DeviceIdType.MESH,
        )

    def outgoing(kind, peer):
        return pltpu.make_async_remote_copy(
            src_ref=moved[kind][0].at[:, cols_of(peer)],
            dst_ref=moved[kind][1].at[rows_of(me), :],
            send_sem=send_sems.at[kind, peer],
            recv_sem=recv_sems.at[kind, me],
            device_id={"head": peer},
            device_id_type=pl.DeviceIdType.MESH,
        )

    def own(kind):
        return pltpu.make_async_copy(
            moved[kind][0].at[:, cols_of(me)], moved[kind][1].at[rows_of(me), :], local_sems.at[kind]
        )

    def total_copy(total, slots, send, recv, far, target):
        return pltpu.make_async_remote_copy(
            src_ref=total,
            dst_ref=slots.at[far - 1],
            send_sem=send.at[far - 1],
            recv_sem=recv.at[far - 1],
            device_id={"seq": target},
            device_id_type=pl.DeviceIdType.MESH,
        )

    def send_totals(total, slots, send, recv):
        for far in range(1, shards):
            @pl.when(shard + far < shards)
            def _():
                total_copy(total, slots, send, recv, far, shard + far).start()

    def wait_totals(total, slots, send, recv):
        for far in range(1, shards):
            @pl.when(shard - far >= 0)
            def _():
                total_copy(total, slots, send, recv, far, shard - far).wait_recv()

    def drain_totals(total, slots, send, recv):
        for far in range(1, shards):
            @pl.when(shard + far < shards)
            def _():
                total_copy(total, slots, send, recv, far, shard + far).wait_send()

    barrier = pltpu.get_barrier_semaphore()
    for step in range(1, owners):
        pl.semaphore_signal(barrier, inc=1, device_id={"head": lax.rem(me + step, owners)}, device_id_type=pl.DeviceIdType.MESH)
    for step in range(1, shards):
        pl.semaphore_signal(barrier, inc=1, device_id={"seq": lax.rem(shard + step, shards)}, device_id_type=pl.DeviceIdType.MESH)
    for kind in range(3):
        own(kind).start()
    pl.semaphore_wait(barrier, owners + shards - 2)
    for kind in range(3):
        for step in range(1, owners):
            outgoing(kind, lax.rem(me + step, owners)).start()
    for kind in range(3):
        own(kind).wait()

    eye = lax.broadcasted_iota(jnp.int32, (DK, DK), 0) == lax.broadcasted_iota(jnp.int32, (DK, DK), 1)
    ridges = [jnp.where(eye, ridge_ref[pl.ds(me * heads + h, 1), :], 0.0) for h in range(heads)]

    def rows_in(source, i):
        return pl.ds(pl.multiple_of(source * rows_each + i * GROUP, GROUP), GROUP)

    def keys_in(source, runs):
        @pl.when(source != me)
        def _():
            incoming(0, source).wait_recv()

        adds = []
        for h in range(heads):
            for i in range(per_source):
                ku = unit(k_all[rows_in(source, i), h * DK : (h + 1) * DK])
                k_all[rows_in(source, i), h * DK : (h + 1) * DK] = ku
                adds.append(dot(ku, ku, (0, 0)))
        runs = list(runs)
        for h in range(heads):
            for i in range(per_source):
                sys_ref[h * groups + source * per_source + i] = runs[h] + ridges[h]
                runs[h] = runs[h] + adds[h * per_source + i]
        return tuple(runs)

    zero = tuple(jnp.zeros((DK, DK), F32) for _ in range(heads))
    runs = lax.fori_loop(0, owners, keys_in, zero)
    for h in range(heads):
        gram_total[h] = runs[h]
    send_totals(gram_total, gram_slots, gram_send, gram_recv)

    def values_in(source, runs):
        @pl.when(source != me)
        def _():
            incoming(1, source).wait_recv()

        adds = []
        for h in range(heads):
            for i in range(per_source):
                cols = slice(h * DK, (h + 1) * DK)
                adds.append(dot(k_all[rows_in(source, i), cols], v_all[rows_in(source, i), cols], (0, 0)))
        runs = list(runs)
        for h in range(heads):
            for i in range(per_source):
                vk_ref[h * groups + source * per_source + i] = runs[h]
                runs[h] = runs[h] + adds[h * per_source + i]
        return tuple(runs)

    runs = lax.fori_loop(0, owners, values_in, zero)
    for h in range(heads):
        vk_total[h] = runs[h]
    send_totals(vk_total, vk_slots, vk_send, vk_recv)

    def sum_slots(slots, total):
        for h in range(heads):
            total[h] = jnp.zeros((DK, DK), F32)
        for far in range(1, shards):
            @pl.when(shard - far >= 0)
            def _():
                for h in range(heads):
                    total[h] = total[h] + slots[far - 1, h]

    wait_totals(gram_total, gram_slots, gram_send, gram_recv)
    drain_totals(gram_total, gram_slots, gram_send, gram_recv)
    sum_slots(gram_slots, gram_total)
    for h in range(heads):
        extra = gram_total[h]

        def add(c, carry):
            sys_ref[h * groups + c] = sys_ref[h * groups + c] + extra
            return carry

        lax.fori_loop(0, groups, add, 0)

    invert_all(sys_ref, pinv_ref)

    wait_totals(vk_total, vk_slots, vk_send, vk_recv)
    drain_totals(vk_total, vk_slots, vk_send, vk_recv)
    sum_slots(vk_slots, vk_total)
    for step in range(1, owners):
        incoming(2, lax.rem(me + step, owners)).wait_recv()

    def result_copy(peer):
        return pltpu.make_async_remote_copy(
            src_ref=stage.at[peer],
            dst_ref=out_hbm.at[:, cols_of(me)],
            send_sem=out_send.at[peer],
            recv_sem=out_recv.at[me],
            device_id={"head": peer},
            device_id_type=pl.DeviceIdType.MESH,
        )

    sub = lax.broadcasted_iota(jnp.int32, (GROUP, 2 * GROUP), 0)
    lane = lax.broadcasted_iota(jnp.int32, (GROUP, 2 * GROUP), 1)
    twice = lane >= GROUP
    causal = jnp.where(twice, lane - GROUP, lane) <= sub

    def finish(step, carry):
        source = lax.rem(me + 1 + step, owners)
        jobs = [(h, i) for h in range(heads) for i in range(per_source)]
        solved = []
        for h, i in jobs:
            qu = unit(q_all[rows_in(source, i), h * DK : (h + 1) * DK])
            full = jnp.concatenate(split3(sys_ref[h * groups + source * per_source + i]), axis=0)
            solved.append(split3(-dot(jnp.concatenate([qu, qu, qu], axis=1), full, (1, 0))))
        scores, carried = [], []
        for (h, i), (high, mid, low) in zip(jobs, solved):
            ku = k_all[rows_in(source, i), h * DK : (h + 1) * DK]
            ku = jnp.concatenate([ku, ku], axis=0)
            ku = jnp.concatenate([ku, ku, ku], axis=1)
            scores.append(dot(jnp.concatenate([high, mid, low], axis=1), ku, (1, 1)))
            left = jnp.concatenate([high, high, mid, high, low, mid], axis=1)
            start = vk_ref[h * groups + source * per_source + i] + vk_total[h]
            carried.append(dot(left, right_stack(split3(start)), (1, 0)))
        for (h, i), score, carry_in in zip(jobs, scores, carried):
            score = jnp.where(causal, score, 0.0)
            high = score.astype(BF16).astype(F32)
            both = jnp.where(twice, score - high, high).astype(BF16)
            vb = v_all[rows_in(source, i), h * DK : (h + 1) * DK]
            inner = dot(both, jnp.concatenate([vb, vb], axis=0), (1, 0))
            stage[source, i * GROUP : (i + 1) * GROUP, h * DK : (h + 1) * DK] = (carry_in + inner).astype(BF16)

        @pl.when(source != me)
        def _():
            result_copy(source).start()

        return carry

    lax.fori_loop(0, owners, finish, 0)
    mine = pltpu.make_async_copy(stage.at[me], out_hbm.at[:, cols_of(me)], out_local)
    mine.start()
    for step in range(1, owners):
        peer = lax.rem(me + step, owners)
        for kind in range(3):
            outgoing(kind, peer).wait_send()
        result_copy(peer).wait_send()
    for step in range(1, owners):
        source = lax.rem(me + step, owners)
        pltpu.make_async_remote_copy(
            src_ref=stage.at[source],
            dst_ref=out_hbm.at[:, cols_of(source)],
            send_sem=out_send.at[source],
            recv_sem=out_recv.at[source],
            device_id={"head": source},
            device_id_type=pl.DeviceIdType.MESH,
        ).wait_recv()
    mine.wait()


def body(queries, key_rows, value_rows, ridge_diag):
    owners, shards = lax.axis_size("head"), lax.axis_size("seq")
    rows, columns = queries.shape
    width = columns // owners
    heads = width // DK
    tokens = rows * owners
    systems = heads * (tokens // GROUP)
    anywhere = pl.BlockSpec(memory_space=pl.ANY)
    dma = pltpu.SemaphoreType.DMA
    return pl.pallas_call(
        functools.partial(whole_kernel, owners, shards),
        out_shape=jax.ShapeDtypeStruct((rows, columns), BF16),
        in_specs=[anywhere] * 3 + [pl.BlockSpec(memory_space=pltpu.VMEM)],
        out_specs=anywhere,
        scratch_shapes=[
            pltpu.VMEM((tokens, width), BF16),
            pltpu.VMEM((tokens, width), BF16),
            pltpu.VMEM((tokens, width), BF16),
            pltpu.VMEM((systems, DK, DK), F32),
            pltpu.VMEM((systems, DK, DK), F32),
            pltpu.VMEM((systems // PACK, EDGE, DK), F32),
            pltpu.VMEM((owners, rows, width), BF16),
            pltpu.VMEM((heads, DK, DK), F32),
            pltpu.VMEM((heads, DK, DK), F32),
            pltpu.VMEM((shards - 1, heads, DK, DK), F32),
            pltpu.VMEM((shards - 1, heads, DK, DK), F32),
            dma((3, owners)), dma((3, owners)), dma((3,)),
            dma((owners,)), dma((owners,)), dma,
            dma((shards - 1,)), dma((shards - 1,)), dma((shards - 1,)), dma((shards - 1,)),
        ],
        compiler_params=pltpu.CompilerParams(
            vmem_limit_bytes=48 * 1024 * 1024, collective_id=0, has_side_effects=True
        ),
    )(queries, key_rows, value_rows, ridge_diag)


def solution(mesh):
    in_specs = (P(("seq", "head"), None), P(("seq", "head"), None), P(("seq", "head"), None), P())
    out_specs = P(("seq", "head"), None)
    return jax.shard_map(body, mesh=mesh, in_specs=in_specs, out_specs=out_specs, check_vma=False)
```

```python
import functools

import jax
import jax.numpy as jnp
from jax import lax
from jax.experimental import pallas as pl
from jax.experimental.pallas import tpu as pltpu
from jax.sharding import PartitionSpec as P

DK = 128
GROUP = 64
EDGE = 32
PACK = DK // EDGE
STEP_PACKS = 4
EPS = 1e-06
F32 = jnp.float32
BF16 = jnp.bfloat16


def unit(rows):
    wide = rows.astype(F32)
    back = lax.rsqrt(jnp.sum(wide * wide, axis=-1, keepdims=True) + EPS)
    return (wide * back).astype(BF16)


def split3(value):
    high = value.astype(BF16)
    rest = value - high.astype(F32)
    mid = rest.astype(BF16)
    low = (rest - mid.astype(F32)).astype(BF16)
    return high, mid, low


def dot(left, right, contract):
    return lax.dot_general(left, right, ((contract[:1], contract[1:]), ((), ())), preferred_element_type=F32)


def left_stack(parts):
    high, mid, low = parts
    return jnp.concatenate([high, high, mid, high, low, mid], axis=0)


def right_stack(parts):
    high, mid, low = parts
    return jnp.concatenate([high, mid, high, low, high, mid], axis=0)


def sweep_round(rows, lane, sub, turn):
    base = (lane // EDGE) * EDGE
    within = lane - base

    def take(block, pick):
        return jnp.take_along_axis(block, pick, axis=1, mode="promise_in_bounds")

    j = turn
    at, inner = j // 8, j % 8
    first, second = within == j, within == j + 1
    either = jnp.logical_or(first, second)
    pick1, pick2 = base + j, base + j + 1
    row1 = jnp.broadcast_to(rows[at][inner : inner + 1, :], rows[at].shape)
    row2 = jnp.broadcast_to(rows[at][inner + 1 : inner + 2, :], rows[at].shape)
    a, b, d = take(row1, pick1), take(row1, pick2), take(row2, pick2)
    inv1 = 1.0 / a
    ratio = b * inv1
    inv2 = 1.0 / (d - b * ratio)
    scaled1 = jnp.where(first, -1.0, row1) * inv1
    scaled2 = jnp.where(second, -1.0, jnp.where(first, 0.0, row2) - b * scaled1) * inv2
    scaled1 = jnp.where(second, 0.0, scaled1)
    fresh = []
    for v, block in enumerate(rows):
        col1, col2 = take(block, pick1), take(block, pick2)
        gone = either
        if v == at:
            here1, here2 = sub == inner, sub == inner + 1
            col1 = jnp.where(here1, -1.0, col1)
            col2 = jnp.where(here2, -1.0, jnp.where(here1, 0.0, col2) - col1 * ratio)
            col1 = jnp.where(here2, 0.0, col1)
            gone = jnp.logical_or(either, jnp.logical_or(here1, here2))
        else:
            col2 = col2 - col1 * ratio
        fresh.append(jnp.where(gone, 0.0, block) - col1 * scaled1 - col2 * scaled2)
    return fresh


def invert_all(sys_ref, pinv_ref):
    count = sys_ref.shape[0]
    packs = count // PACK
    lane = lax.broadcasted_iota(jnp.int32, (8, DK), 1)
    sub = lax.broadcasted_iota(jnp.int32, (8, DK), 0)
    lane32 = lax.broadcasted_iota(jnp.int32, (EDGE, DK), 1)
    sub32 = lax.broadcasted_iota(jnp.int32, (EDGE, DK), 0)
    row128 = lax.broadcasted_iota(jnp.int32, (DK, DK), 0) // EDGE
    lane128 = lax.broadcasted_iota(jnp.int32, (DK, DK), 1) // EDGE

    def panel(p, carry):
        start = pl.multiple_of(p * EDGE, EDGE)
        all_rows = []
        for g in range(packs):
            packed = None
            for k in range(PACK):
                piece = sys_ref[g * PACK + k, pl.ds(start, EDGE), :]
                piece = pltpu.roll(piece, lax.rem((k - p) * EDGE + DK, DK), 1)
                packed = piece if packed is None else jnp.where(lane32 // EDGE == k, piece, packed)
            all_rows.append([packed[8 * v : 8 * v + 8, :] for v in range(EDGE // 8)])
        for turn in range(0, EDGE, 2):
            all_rows = [sweep_round(rows, lane, sub, turn) for rows in all_rows]
        for g in range(packs):
            pinv_ref[g] = jnp.concatenate(all_rows[g], axis=0)

        mine = lane32 // EDGE == p
        diag = lane32 - p * EDGE == sub32
        cleared = jnp.logical_or(row128 == p, lane128 == p)

        def update(turn, carry):
            batch = [turn * STEP_PACKS + i for i in range(STEP_PACKS)]
            rows, inverses = [], []
            for g in batch:
                inverses.append(jnp.transpose(left_stack(split3(pinv_ref[g]))))
                for k in range(PACK):
                    rows.append(sys_ref[g * PACK + k, pl.ds(start, EDGE), :])
            rows = [split3(jnp.where(mine, jnp.where(diag, -1.0, 0.0), r)) for r in rows]
            scaled = []
            for i in range(STEP_PACKS):
                for k in range(PACK):
                    left = inverses[i][k * EDGE : (k + 1) * EDGE, :]
                    scaled.append(dot(left, right_stack(rows[i * PACK + k]), (1, 0)))
            change = [dot(left_stack(r), right_stack(split3(t)), (0, 0)) for r, t in zip(rows, scaled)]
            for i, c in enumerate(change):
                s = turn * STEP_PACKS * PACK + i
                sys_ref[s] = jnp.where(cleared, 0.0, sys_ref[s]) + c
            return carry

        return lax.fori_loop(0, packs // STEP_PACKS, update, carry)

    lax.fori_loop(0, PACK, panel, 0)


def whole_kernel(
    owners, shards, q_hbm, k_hbm, v_hbm, ridge_ref, out_hbm,
    q_all, k_all, v_all, sys_ref, vk_ref, pinv_ref, stage, gram_total, vk_total, gram_slots, vk_slots,
    send_sems, recv_sems, local_sems, out_send, out_recv, out_local, gram_send, gram_recv, vk_send, vk_recv,
):
    me, shard = lax.axis_index("head"), lax.axis_index("seq")
    rows_each = q_hbm.shape[0]
    width = q_all.shape[1]
    heads = width // DK
    per_source = rows_each // GROUP
    groups = owners * per_source
    moved = ((k_hbm, k_all), (v_hbm, v_all), (q_hbm, q_all))

    def rows_of(source):
        return pl.ds(pl.multiple_of(source * rows_each, rows_each), rows_each)

    def cols_of(owner):
        return pl.ds(pl.multiple_of(owner * width, width), width)

    def incoming(kind, source):
        return pltpu.make_async_remote_copy(
            src_ref=moved[kind][0].at[:, cols_of(source)],
            dst_ref=moved[kind][1].at[rows_of(source), :],
            send_sem=send_sems.at[kind, source],
            recv_sem=recv_sems.at[kind, source],
            device_id={"head": source},
            device_id_type=pl.DeviceIdType.MESH,
        )

    def outgoing(kind, peer):
        return pltpu.make_async_remote_copy(
            src_ref=moved[kind][0].at[:, cols_of(peer)],
            dst_ref=moved[kind][1].at[rows_of(me), :],
            send_sem=send_sems.at[kind, peer],
            recv_sem=recv_sems.at[kind, me],
            device_id={"head": peer},
            device_id_type=pl.DeviceIdType.MESH,
        )

    def own(kind):
        return pltpu.make_async_copy(
            moved[kind][0].at[:, cols_of(me)], moved[kind][1].at[rows_of(me), :], local_sems.at[kind]
        )

    def total_copy(total, slots, send, recv, far, target):
        return pltpu.make_async_remote_copy(
            src_ref=total,
            dst_ref=slots.at[far - 1],
            send_sem=send.at[far - 1],
            recv_sem=recv.at[far - 1],
            device_id={"seq": target},
            device_id_type=pl.DeviceIdType.MESH,
        )

    def send_totals(total, slots, send, recv):
        for far in reversed(range(1, shards)):
            @pl.when(shard + far < shards)
            def _():
                total_copy(total, slots, send, recv, far, shard + far).start()

    def wait_totals(total, slots, send, recv):
        for far in range(1, shards):
            @pl.when(shard - far >= 0)
            def _():
                total_copy(total, slots, send, recv, far, shard - far).wait_recv()

    def drain_totals(total, slots, send, recv):
        for far in range(1, shards):
            @pl.when(shard + far < shards)
            def _():
                total_copy(total, slots, send, recv, far, shard + far).wait_send()

    barrier = pltpu.get_barrier_semaphore()
    for step in range(1, owners):
        pl.semaphore_signal(barrier, inc=1, device_id={"head": lax.rem(me + step, owners)}, device_id_type=pl.DeviceIdType.MESH)
    for step in range(1, shards):
        pl.semaphore_signal(barrier, inc=1, device_id={"seq": lax.rem(shard + step, shards)}, device_id_type=pl.DeviceIdType.MESH)
    for kind in range(3):
        own(kind).start()
    pl.semaphore_wait(barrier, owners + shards - 2)
    for kind in range(3):
        for step in range(1, owners):
            outgoing(kind, lax.rem(me + step, owners)).start()
    for kind in range(3):
        own(kind).wait()

    eye = lax.broadcasted_iota(jnp.int32, (DK, DK), 0) == lax.broadcasted_iota(jnp.int32, (DK, DK), 1)
    ridges = [jnp.where(eye, ridge_ref[pl.ds(me * heads + h, 1), :], 0.0) for h in range(heads)]

    def rows_in(source, i):
        return pl.ds(pl.multiple_of(source * rows_each + i * GROUP, GROUP), GROUP)

    def keys_in(source, runs):
        @pl.when(source != me)
        def _():
            incoming(0, source).wait_recv()

        adds = []
        for h in range(heads):
            for i in range(per_source):
                ku = unit(k_all[rows_in(source, i), h * DK : (h + 1) * DK])
                k_all[rows_in(source, i), h * DK : (h + 1) * DK] = ku
                adds.append(dot(ku, ku, (0, 0)))
        runs = list(runs)
        for h in range(heads):
            for i in range(per_source):
                sys_ref[h * groups + source * per_source + i] = runs[h] + ridges[h]
                runs[h] = runs[h] + adds[h * per_source + i]
        return tuple(runs)

    zero = tuple(jnp.zeros((DK, DK), F32) for _ in range(heads))
    runs = lax.fori_loop(0, owners, keys_in, zero)
    for h in range(heads):
        gram_total[h] = runs[h]
    send_totals(gram_total, gram_slots, gram_send, gram_recv)

    def values_in(source, runs):
        @pl.when(source != me)
        def _():
            incoming(1, source).wait_recv()

        adds = []
        for h in range(heads):
            for i in range(per_source):
                cols = slice(h * DK, (h + 1) * DK)
                adds.append(dot(k_all[rows_in(source, i), cols], v_all[rows_in(source, i), cols], (0, 0)))
        runs = list(runs)
        for h in range(heads):
            for i in range(per_source):
                vk_ref[h * groups + source * per_source + i] = runs[h]
                runs[h] = runs[h] + adds[h * per_source + i]
        return tuple(runs)

    runs = lax.fori_loop(0, owners, values_in, zero)
    for h in range(heads):
        vk_total[h] = runs[h]
    send_totals(vk_total, vk_slots, vk_send, vk_recv)

    def sum_slots(slots, total):
        for h in range(heads):
            total[h] = jnp.zeros((DK, DK), F32)
        for far in range(1, shards):
            @pl.when(shard - far >= 0)
            def _():
                for h in range(heads):
                    total[h] = total[h] + slots[far - 1, h]

    wait_totals(gram_total, gram_slots, gram_send, gram_recv)
    drain_totals(gram_total, gram_slots, gram_send, gram_recv)
    sum_slots(gram_slots, gram_total)
    for h in range(heads):
        extra = gram_total[h]

        def add(c, carry):
            sys_ref[h * groups + c] = sys_ref[h * groups + c] + extra
            return carry

        lax.fori_loop(0, groups, add, 0)

    invert_all(sys_ref, pinv_ref)

    wait_totals(vk_total, vk_slots, vk_send, vk_recv)
    drain_totals(vk_total, vk_slots, vk_send, vk_recv)
    sum_slots(vk_slots, vk_total)
    for step in range(1, owners):
        incoming(2, lax.rem(me + step, owners)).wait_recv()

    def result_copy(peer):
        return pltpu.make_async_remote_copy(
            src_ref=stage.at[peer],
            dst_ref=out_hbm.at[:, cols_of(me)],
            send_sem=out_send.at[peer],
            recv_sem=out_recv.at[me],
            device_id={"head": peer},
            device_id_type=pl.DeviceIdType.MESH,
        )

    sub = lax.broadcasted_iota(jnp.int32, (GROUP, 2 * GROUP), 0)
    lane = lax.broadcasted_iota(jnp.int32, (GROUP, 2 * GROUP), 1)
    twice = lane >= GROUP
    causal = jnp.where(twice, lane - GROUP, lane) <= sub

    def finish(step, carry):
        source = lax.rem(me + 1 + step, owners)
        jobs = [(h, i) for h in range(heads) for i in range(per_source)]
        solved = []
        for h, i in jobs:
            qu = unit(q_all[rows_in(source, i), h * DK : (h + 1) * DK])
            full = jnp.concatenate(split3(sys_ref[h * groups + source * per_source + i]), axis=0)
            solved.append(split3(-dot(jnp.concatenate([qu, qu, qu], axis=1), full, (1, 0))))
        scores, carried = [], []
        for (h, i), (high, mid, low) in zip(jobs, solved):
            ku = k_all[rows_in(source, i), h * DK : (h + 1) * DK]
            ku = jnp.concatenate([ku, ku], axis=0)
            ku = jnp.concatenate([ku, ku, ku], axis=1)
            scores.append(dot(jnp.concatenate([high, mid, low], axis=1), ku, (1, 1)))
            left = jnp.concatenate([high, high, mid, high, low, mid], axis=1)
            start = vk_ref[h * groups + source * per_source + i] + vk_total[h]
            carried.append(dot(left, right_stack(split3(start)), (1, 0)))
        for (h, i), score, carry_in in zip(jobs, scores, carried):
            score = jnp.where(causal, score, 0.0)
            high = score.astype(BF16).astype(F32)
            both = jnp.where(twice, score - high, high).astype(BF16)
            vb = v_all[rows_in(source, i), h * DK : (h + 1) * DK]
            inner = dot(both, jnp.concatenate([vb, vb], axis=0), (1, 0))
            stage[source, i * GROUP : (i + 1) * GROUP, h * DK : (h + 1) * DK] = (carry_in + inner).astype(BF16)

        @pl.when(source != me)
        def _():
            result_copy(source).start()

        return carry

    lax.fori_loop(0, owners, finish, 0)
    mine = pltpu.make_async_copy(stage.at[me], out_hbm.at[:, cols_of(me)], out_local)
    mine.start()
    for step in range(1, owners):
        peer = lax.rem(me + step, owners)
        for kind in range(3):
            outgoing(kind, peer).wait_send()
        result_copy(peer).wait_send()
    for step in range(1, owners):
        source = lax.rem(me + step, owners)
        pltpu.make_async_remote_copy(
            src_ref=stage.at[source],
            dst_ref=out_hbm.at[:, cols_of(source)],
            send_sem=out_send.at[source],
            recv_sem=out_recv.at[source],
            device_id={"head": source},
            device_id_type=pl.DeviceIdType.MESH,
        ).wait_recv()
    mine.wait()


def body(queries, key_rows, value_rows, ridge_diag):
    owners, shards = lax.axis_size("head"), lax.axis_size("seq")
    rows, columns = queries.shape
    width = columns // owners
    heads = width // DK
    tokens = rows * owners
    systems = heads * (tokens // GROUP)
    anywhere = pl.BlockSpec(memory_space=pltpu.HBM)
    dma = pltpu.SemaphoreType.DMA
    return pl.pallas_call(
        functools.partial(whole_kernel, owners, shards),
        out_shape=jax.ShapeDtypeStruct((rows, columns), BF16),
        in_specs=[anywhere] * 3 + [pl.BlockSpec(memory_space=pltpu.VMEM)],
        out_specs=anywhere,
        scratch_shapes=[
            pltpu.VMEM((tokens, width), BF16),
            pltpu.VMEM((tokens, width), BF16),
            pltpu.VMEM((tokens, width), BF16),
            pltpu.VMEM((systems, DK, DK), F32),
            pltpu.VMEM((systems, DK, DK), F32),
            pltpu.VMEM((systems // PACK, EDGE, DK), F32),
            pltpu.VMEM((owners, rows, width), BF16),
            pltpu.VMEM((heads, DK, DK), F32),
            pltpu.VMEM((heads, DK, DK), F32),
            pltpu.VMEM((shards - 1, heads, DK, DK), F32),
            pltpu.VMEM((shards - 1, heads, DK, DK), F32),
            dma((3, owners)), dma((3, owners)), dma((3,)),
            dma((owners,)), dma((owners,)), dma,
            dma((shards - 1,)), dma((shards - 1,)), dma((shards - 1,)), dma((shards - 1,)),
        ],
        compiler_params=pltpu.CompilerParams(
            vmem_limit_bytes=67_000_000, collective_id=0, has_side_effects=True
        ),
    )(queries, key_rows, value_rows, ridge_diag)


def solution(mesh):
    in_specs = (P(("seq", "head"), None), P(("seq", "head"), None), P(("seq", "head"), None), P())
    out_specs = P(("seq", "head"), None)
    return jax.shard_map(body, mesh=mesh, in_specs=in_specs, out_specs=out_specs, check_vma=False)
```

```python
import functools

import jax
import jax.numpy as jnp
from jax import lax
from jax.experimental import pallas as pl
from jax.experimental.pallas import tpu as pltpu
from jax.sharding import PartitionSpec as P

DK = 128
GROUP = 64
EDGE = 32
PACK = DK // EDGE
STEP_PACKS = 4
EPS = 1e-06
F32 = jnp.float32
BF16 = jnp.bfloat16


def unit(rows):
    wide = rows.astype(F32)
    back = lax.rsqrt(jnp.sum(wide * wide, axis=-1, keepdims=True) + EPS)
    return (wide * back).astype(BF16)


def split3(value):
    high = value.astype(BF16)
    rest = value - high.astype(F32)
    mid = rest.astype(BF16)
    low = (rest - mid.astype(F32)).astype(BF16)
    return high, mid, low


def dot(left, right, contract):
    return lax.dot_general(left, right, ((contract[:1], contract[1:]), ((), ())), preferred_element_type=F32)


def left_stack(parts):
    high, mid, low = parts
    return jnp.concatenate([high, high, mid, high, low, mid], axis=0)


def right_stack(parts):
    high, mid, low = parts
    return jnp.concatenate([high, mid, high, low, high, mid], axis=0)


def sweep_round(rows, lane, sub, turn):
    base = (lane // EDGE) * EDGE
    within = lane - base

    def take(block, pick):
        return jnp.take_along_axis(block, pick, axis=1, mode="promise_in_bounds")

    j = turn
    at, inner = j // 8, j % 8
    first, second = within == j, within == j + 1
    either = jnp.logical_or(first, second)
    pick1, pick2 = base + j, base + j + 1
    row1 = jnp.broadcast_to(rows[at][inner : inner + 1, :], rows[at].shape)
    row2 = jnp.broadcast_to(rows[at][inner + 1 : inner + 2, :], rows[at].shape)
    a, b, d = take(row1, pick1), take(row1, pick2), take(row2, pick2)
    inv1 = 1.0 / a
    ratio = b * inv1
    inv2 = 1.0 / (d - b * ratio)
    scaled1 = jnp.where(first, -1.0, row1) * inv1
    scaled2 = jnp.where(second, -1.0, jnp.where(first, 0.0, row2) - b * scaled1) * inv2
    scaled1 = jnp.where(second, 0.0, scaled1)
    fresh = []
    for v, block in enumerate(rows):
        col1, col2 = take(block, pick1), take(block, pick2)
        gone = either
        if v == at:
            here1, here2 = sub == inner, sub == inner + 1
            col1 = jnp.where(here1, -1.0, col1)
            col2 = jnp.where(here2, -1.0, jnp.where(here1, 0.0, col2) - col1 * ratio)
            col1 = jnp.where(here2, 0.0, col1)
            gone = jnp.logical_or(either, jnp.logical_or(here1, here2))
        else:
            col2 = col2 - col1 * ratio
        fresh.append(jnp.where(gone, 0.0, block) - col1 * scaled1 - col2 * scaled2)
    return fresh


def invert_all(sys_ref, pinv_ref, after_first):
    count = sys_ref.shape[0]
    packs = count // PACK
    lane = lax.broadcasted_iota(jnp.int32, (8, DK), 1)
    sub = lax.broadcasted_iota(jnp.int32, (8, DK), 0)
    lane32 = lax.broadcasted_iota(jnp.int32, (EDGE, DK), 1)
    sub32 = lax.broadcasted_iota(jnp.int32, (EDGE, DK), 0)
    row128 = lax.broadcasted_iota(jnp.int32, (DK, DK), 0) // EDGE
    lane128 = lax.broadcasted_iota(jnp.int32, (DK, DK), 1) // EDGE

    def panel(p, carry):
        @pl.when(p == 1)
        def _():
            after_first()

        start = pl.multiple_of(p * EDGE, EDGE)
        all_rows = []
        for g in range(packs):
            packed = None
            for k in range(PACK):
                piece = sys_ref[g * PACK + k, pl.ds(start, EDGE), :]
                piece = pltpu.roll(piece, lax.rem((k - p) * EDGE + DK, DK), 1)
                packed = piece if packed is None else jnp.where(lane32 // EDGE == k, piece, packed)
            all_rows.append([packed[8 * v : 8 * v + 8, :] for v in range(EDGE // 8)])
        for turn in range(0, EDGE, 2):
            all_rows = [sweep_round(rows, lane, sub, turn) for rows in all_rows]
        for g in range(packs):
            pinv_ref[g] = jnp.concatenate(all_rows[g], axis=0)

        mine = lane32 // EDGE == p
        diag = lane32 - p * EDGE == sub32
        cleared = jnp.logical_or(row128 == p, lane128 == p)

        def update(turn, carry):
            batch = [turn * STEP_PACKS + i for i in range(STEP_PACKS)]
            rows, inverses = [], []
            for g in batch:
                inverses.append(jnp.transpose(left_stack(split3(pinv_ref[g]))))
                for k in range(PACK):
                    rows.append(sys_ref[g * PACK + k, pl.ds(start, EDGE), :])
            rows = [split3(jnp.where(mine, jnp.where(diag, -1.0, 0.0), r)) for r in rows]
            scaled = []
            for i in range(STEP_PACKS):
                for k in range(PACK):
                    left = inverses[i][k * EDGE : (k + 1) * EDGE, :]
                    scaled.append(dot(left, right_stack(rows[i * PACK + k]), (1, 0)))
            change = [dot(left_stack(r), right_stack(split3(t)), (0, 0)) for r, t in zip(rows, scaled)]
            for i, c in enumerate(change):
                s = turn * STEP_PACKS * PACK + i
                sys_ref[s] = jnp.where(cleared, 0.0, sys_ref[s]) + c
            return carry

        return lax.fori_loop(0, packs // STEP_PACKS, update, carry)

    lax.fori_loop(0, PACK, panel, 0)


def whole_kernel(
    owners, shards, q_hbm, k_hbm, v_hbm, ridge_ref, out_hbm,
    q_all, k_all, v_all, sys_ref, vk_ref, pinv_ref, stage, before, gram_total, vk_total, gram_slots, vk_slots,
    send_sems, recv_sems, local_sems, out_send, out_recv, out_local, gram_send, gram_recv, vk_send, vk_recv,
):
    me, shard = lax.axis_index("head"), lax.axis_index("seq")
    rows_each = q_hbm.shape[0]
    width = q_all.shape[1]
    heads = width // DK
    per_source = rows_each // GROUP
    groups = owners * per_source
    moved = ((k_hbm, k_all), (v_hbm, v_all), (q_hbm, q_all))

    def rows_of(source):
        return pl.ds(pl.multiple_of(source * rows_each, rows_each), rows_each)

    def cols_of(owner):
        return pl.ds(pl.multiple_of(owner * width, width), width)

    def incoming(kind, source):
        return pltpu.make_async_remote_copy(
            src_ref=moved[kind][0].at[:, cols_of(source)],
            dst_ref=moved[kind][1].at[rows_of(source), :],
            send_sem=send_sems.at[kind, source],
            recv_sem=recv_sems.at[kind, source],
            device_id={"head": source},
            device_id_type=pl.DeviceIdType.MESH,
        )

    def outgoing(kind, peer):
        return pltpu.make_async_remote_copy(
            src_ref=moved[kind][0].at[:, cols_of(peer)],
            dst_ref=moved[kind][1].at[rows_of(me), :],
            send_sem=send_sems.at[kind, peer],
            recv_sem=recv_sems.at[kind, me],
            device_id={"head": peer},
            device_id_type=pl.DeviceIdType.MESH,
        )

    def own(kind):
        return pltpu.make_async_copy(
            moved[kind][0].at[:, cols_of(me)], moved[kind][1].at[rows_of(me), :], local_sems.at[kind]
        )

    def total_copy(total, slots, send, recv, far, target):
        return pltpu.make_async_remote_copy(
            src_ref=total,
            dst_ref=slots.at[far - 1],
            send_sem=send.at[far - 1],
            recv_sem=recv.at[far - 1],
            device_id={"seq": target},
            device_id_type=pl.DeviceIdType.MESH,
        )

    def send_totals(total, slots, send, recv):
        for far in range(1, shards):
            @pl.when(shard + far < shards)
            def _():
                total_copy(total, slots, send, recv, far, shard + far).start()

    def wait_totals(total, slots, send, recv):
        for far in range(1, shards):
            @pl.when(shard - far >= 0)
            def _():
                total_copy(total, slots, send, recv, far, shard - far).wait_recv()

    def drain_totals(total, slots, send, recv):
        for far in range(1, shards):
            @pl.when(shard + far < shards)
            def _():
                total_copy(total, slots, send, recv, far, shard + far).wait_send()

    barrier = pltpu.get_barrier_semaphore()
    for step in range(1, owners):
        pl.semaphore_signal(barrier, inc=1, device_id={"head": lax.rem(me + step, owners)}, device_id_type=pl.DeviceIdType.MESH)
    for step in range(1, shards):
        pl.semaphore_signal(barrier, inc=1, device_id={"seq": lax.rem(shard + step, shards)}, device_id_type=pl.DeviceIdType.MESH)
    for kind in range(3):
        own(kind).start()
    pl.semaphore_wait(barrier, owners + shards - 2)
    for kind in range(3):
        for step in range(1, owners):
            outgoing(kind, lax.rem(me + step, owners)).start()
    for kind in range(3):
        own(kind).wait()

    eye = lax.broadcasted_iota(jnp.int32, (DK, DK), 0) == lax.broadcasted_iota(jnp.int32, (DK, DK), 1)
    ridges = [jnp.where(eye, ridge_ref[pl.ds(me * heads + h, 1), :], 0.0) for h in range(heads)]

    def rows_in(source, i):
        return pl.ds(pl.multiple_of(source * rows_each + i * GROUP, GROUP), GROUP)

    def keys_in(source, runs):
        @pl.when(source != me)
        def _():
            incoming(0, source).wait_recv()

        adds = []
        for h in range(heads):
            for i in range(per_source):
                ku = unit(k_all[rows_in(source, i), h * DK : (h + 1) * DK])
                k_all[rows_in(source, i), h * DK : (h + 1) * DK] = ku
                adds.append(dot(ku, ku, (0, 0)))
        runs = list(runs)
        for h in range(heads):
            for i in range(per_source):
                sys_ref[h * groups + source * per_source + i] = runs[h] + ridges[h]
                runs[h] = runs[h] + adds[h * per_source + i]
        return tuple(runs)

    zero = tuple(jnp.zeros((DK, DK), F32) for _ in range(heads))
    runs = lax.fori_loop(0, owners, keys_in, zero)
    for h in range(heads):
        gram_total[h] = runs[h]
    send_totals(gram_total, gram_slots, gram_send, gram_recv)

    def values_in(source, runs):
        @pl.when(source != me)
        def _():
            incoming(1, source).wait_recv()

        adds = []
        for h in range(heads):
            for i in range(per_source):
                cols = slice(h * DK, (h + 1) * DK)
                adds.append(dot(k_all[rows_in(source, i), cols], v_all[rows_in(source, i), cols], (0, 0)))
        runs = list(runs)
        for h in range(heads):
            for i in range(per_source):
                vk_ref[h * groups + source * per_source + i] = runs[h]
                runs[h] = runs[h] + adds[h * per_source + i]
        return tuple(runs)

    runs = lax.fori_loop(0, owners, values_in, zero)
    for h in range(heads):
        vk_total[h] = runs[h]

    def sum_slots(slots, total):
        for h in range(heads):
            total[h] = jnp.zeros((DK, DK), F32)
        for far in range(1, shards):
            @pl.when(shard - far >= 0)
            def _():
                for h in range(heads):
                    total[h] = total[h] + slots[far - 1, h]

    wait_totals(gram_total, gram_slots, gram_send, gram_recv)
    sum_slots(gram_slots, before)
    for h in range(heads):
        extra = before[h]

        def add(c, carry):
            sys_ref[h * groups + c] = sys_ref[h * groups + c] + extra
            return carry

        lax.fori_loop(0, groups, add, 0)

    invert_all(sys_ref, pinv_ref, lambda: send_totals(vk_total, vk_slots, vk_send, vk_recv))

    wait_totals(vk_total, vk_slots, vk_send, vk_recv)
    sum_slots(vk_slots, before)
    for step in range(1, owners):
        incoming(2, lax.rem(me + step, owners)).wait_recv()

    def result_copy(peer):
        return pltpu.make_async_remote_copy(
            src_ref=stage.at[peer],
            dst_ref=out_hbm.at[:, cols_of(me)],
            send_sem=out_send.at[peer],
            recv_sem=out_recv.at[me],
            device_id={"head": peer},
            device_id_type=pl.DeviceIdType.MESH,
        )

    sub = lax.broadcasted_iota(jnp.int32, (GROUP, 2 * GROUP), 0)
    lane = lax.broadcasted_iota(jnp.int32, (GROUP, 2 * GROUP), 1)
    twice = lane >= GROUP
    causal = jnp.where(twice, lane - GROUP, lane) <= sub

    def finish(step, carry):
        source = lax.rem(me + 1 + step, owners)
        jobs = [(h, i) for h in range(heads) for i in range(per_source)]
        solved = []
        for h, i in jobs:
            qu = unit(q_all[rows_in(source, i), h * DK : (h + 1) * DK])
            full = jnp.concatenate(split3(sys_ref[h * groups + source * per_source + i]), axis=0)
            solved.append(split3(-dot(jnp.concatenate([qu, qu, qu], axis=1), full, (1, 0))))
        scores, carried = [], []
        for (h, i), (high, mid, low) in zip(jobs, solved):
            ku = k_all[rows_in(source, i), h * DK : (h + 1) * DK]
            ku = jnp.concatenate([ku, ku], axis=0)
            ku = jnp.concatenate([ku, ku, ku], axis=1)
            scores.append(dot(jnp.concatenate([high, mid, low], axis=1), ku, (1, 1)))
            left = jnp.concatenate([high, high, mid, high, low, mid], axis=1)
            start = vk_ref[h * groups + source * per_source + i] + before[h]
            carried.append(dot(left, right_stack(split3(start)), (1, 0)))
        for (h, i), score, carry_in in zip(jobs, scores, carried):
            score = jnp.where(causal, score, 0.0)
            high = score.astype(BF16).astype(F32)
            both = jnp.where(twice, score - high, high).astype(BF16)
            vb = v_all[rows_in(source, i), h * DK : (h + 1) * DK]
            inner = dot(both, jnp.concatenate([vb, vb], axis=0), (1, 0))
            stage[source, i * GROUP : (i + 1) * GROUP, h * DK : (h + 1) * DK] = (carry_in + inner).astype(BF16)

        @pl.when(source != me)
        def _():
            result_copy(source).start()

        return carry

    lax.fori_loop(0, owners, finish, 0)
    mine = pltpu.make_async_copy(stage.at[me], out_hbm.at[:, cols_of(me)], out_local)
    mine.start()
    for step in range(1, owners):
        peer = lax.rem(me + step, owners)
        for kind in range(3):
            outgoing(kind, peer).wait_send()
        result_copy(peer).wait_send()
    for step in range(1, owners):
        source = lax.rem(me + step, owners)
        pltpu.make_async_remote_copy(
            src_ref=stage.at[source],
            dst_ref=out_hbm.at[:, cols_of(source)],
            send_sem=out_send.at[source],
            recv_sem=out_recv.at[source],
            device_id={"head": source},
            device_id_type=pl.DeviceIdType.MESH,
        ).wait_recv()
    mine.wait()
    drain_totals(gram_total, gram_slots, gram_send, gram_recv)
    drain_totals(vk_total, vk_slots, vk_send, vk_recv)


def body(queries, key_rows, value_rows, ridge_diag):
    owners, shards = lax.axis_size("head"), lax.axis_size("seq")
    rows, columns = queries.shape
    width = columns // owners
    heads = width // DK
    tokens = rows * owners
    systems = heads * (tokens // GROUP)
    anywhere = pl.BlockSpec(memory_space=pltpu.HBM)
    dma = pltpu.SemaphoreType.DMA
    return pl.pallas_call(
        functools.partial(whole_kernel, owners, shards),
        out_shape=jax.ShapeDtypeStruct((rows, columns), BF16),
        in_specs=[anywhere] * 3 + [pl.BlockSpec(memory_space=pltpu.VMEM)],
        out_specs=anywhere,
        scratch_shapes=[
            pltpu.VMEM((tokens, width), BF16),
            pltpu.VMEM((tokens, width), BF16),
            pltpu.VMEM((tokens, width), BF16),
            pltpu.VMEM((systems, DK, DK), F32),
            pltpu.VMEM((systems, DK, DK), F32),
            pltpu.VMEM((systems // PACK, EDGE, DK), F32),
            pltpu.VMEM((owners, rows, width), BF16),
            pltpu.VMEM((heads, DK, DK), F32),
            pltpu.VMEM((heads, DK, DK), F32),
            pltpu.VMEM((heads, DK, DK), F32),
            pltpu.VMEM((shards - 1, heads, DK, DK), F32),
            pltpu.VMEM((shards - 1, heads, DK, DK), F32),
            dma((3, owners)), dma((3, owners)), dma((3,)),
            dma((owners,)), dma((owners,)), dma,
            dma((shards - 1,)), dma((shards - 1,)), dma((shards - 1,)), dma((shards - 1,)),
        ],
        compiler_params=pltpu.CompilerParams(
            vmem_limit_bytes=67_000_000, collective_id=0, has_side_effects=True
        ),
    )(queries, key_rows, value_rows, ridge_diag)


def solution(mesh):
    in_specs = (P(("seq", "head"), None), P(("seq", "head"), None), P(("seq", "head"), None), P())
    out_specs = P(("seq", "head"), None)
    return jax.shard_map(body, mesh=mesh, in_specs=in_specs, out_specs=out_specs, check_vma=False)
```
